32 devices in a mesh: gx: 2 (over y), gy: 4 (over x, core), gz: 4 (over z).
Axes of the slice: x: 2, y: 2, z: 4, core: 2. Of those that a mesh axis runs over, the one named last changes fastest.
Arguments:
- weights: bfloat16 [2, 216, 16384], P(None, None, ('gx', 'gy', 'gz')), may hold values from -6 to 6
- translate: bfloat16 [2, 2, 216, 216], replicated, may hold values from -0.3125 to 0.3125
- angles: float32 [216, 256], replicated, may hold values from -3.140625 to 3.140625
- box_ids: int32 [5, 16384], P(None, ('gx', 'gy', 'gz')), may hold values from 0 to 255
Outputs:
- transformed: bfloat16 [2, 216, 16384], P(None, None, ('gx', 'gy', 'gz'))
The draws below stay inside these ranges and needn't reach their ends.
All inputs are finite; a program needn't handle non-finite values.
Results may differ from the reference program's by a relative error of at most 0.018.
Values may be sent and summed in bfloat16 or wider, within the bound.
A program may use at most 64 MiB of HBM per device.

```python
import jax
import jax.numpy as jnp
from jax import lax

K = 216
NBOX = 256
P_DEV = 512
LEVELS = 5
PTOT = 16384
N_GX = 2
N_GY = 4
N_GZ = 4


def touch_ends(array, stream_key, low, top_value):
    spot = [jax.random.randint(jax.random.fold_in(stream_key, axis), (), 0, length) for axis, length in enumerate(array.shape)]
    longest = array.shape.index(max(array.shape))
    beside = spot[:longest] + [(spot[longest] + 1) % array.shape[longest]] + spot[longest + 1:]
    return array.at[tuple(spot)].set(low).at[tuple(beside)].set(top_value)


def block_levels(key, extent, cuts, low, largest):
    def one(axis_at, parts):
        steps = jax.random.uniform(jax.random.fold_in(jax.random.fold_in(key, 6), axis_at), (parts,), jnp.float32, low / len(cuts), largest / len(cuts))
        return jnp.repeat(jnp.exp(steps), extent[axis_at] // parts).reshape((-1,) + (1,) * (len(extent) - axis_at - 1))

    loudness = one(*cuts[0])
    for cut in cuts[1:]:
        loudness = loudness * one(*cut)
    return loudness


def noise(rng, extent, scale, reach, shards=(), dtype=jnp.bfloat16):
    array = jax.random.normal(rng, extent, jnp.float32) * scale
    if len(shards) > 0:
        array = block_levels(rng, extent, shards, -0.22, 0.18) * array
    return jnp.clip(array, min=-reach, max=reach).astype(dtype)


def setup_inputs(seed: int = 0) -> dict:
    arg_keys = jax.random.split(jax.random.key(seed), 5)
    return {
        "weights": noise(arg_keys[0], (2, K, PTOT), 1.0, 6.0, ((2, 32),)),
        "translate": noise(arg_keys[1], (2, 2, K, K), (2 * K) ** -0.5, 0.3125),
        "angles": jnp.clip(jax.random.uniform(arg_keys[2], (K, NBOX), jnp.float32, -3.140625, 3.140625), -3.140625, 3.140625),
        "box_ids": touch_ends(jax.random.randint(arg_keys[3], (LEVELS, PTOT), 0, NBOX), jax.random.fold_in(arg_keys[3], 1), 0, NBOX - 1).astype(jnp.int32),
    }


def rotate(current, labels, cos_tab, sin_tab):
    cosines = jnp.take(cos_tab, labels, axis=1)
    sines = jnp.take(sin_tab, labels, axis=1)
    real_part = current[0].astype(jnp.float32)
    imag_part = current[1].astype(jnp.float32)
    return jnp.stack([cosines * real_part - sines * imag_part, sines * real_part + cosines * imag_part]).astype(jnp.bfloat16)


def reference(weights, translate, angles, box_ids):
    cos_tab = jnp.cos(angles)
    sin_tab = jnp.sin(angles)
    devices_all = N_GX * N_GY * N_GZ
    current = weights
    level_index = 0
    matrices = translate.astype(jnp.float32)
    for axis_size, stride in ((N_GX, N_GY * N_GZ), (N_GY, N_GZ), (N_GZ, 1)):
        for bit_no in range(axis_size.bit_length() - 1):
            low_size = stride * (1 << bit_no)
            rotated = rotate(current, box_ids[level_index], cos_tab, sin_tab)
            blocked = rotated.reshape(2, K, devices_all // (2 * low_size), 2, low_size, 2, P_DEV // 2).astype(jnp.float32)
            mixed = jnp.einsum('tcjk,rkacbvi->rjavbti', matrices, blocked, precision=lax.Precision.HIGHEST)
            current = mixed.reshape(2, K, -1).astype(jnp.bfloat16)
            level_index += 1
    return current
```

```python
import functools

import jax
import jax.numpy as jnp
from jax import lax
from jax.experimental import pallas as pl
from jax.experimental.pallas import tpu as pltpu
from jax.sharding import PartitionSpec as P

AXES = ("gx", "gy", "gz")
MESH = pl.DeviceIdType.MESH
LANES = 128


def sin_cos(x):
    turn = jnp.floor(x * 0.6366197723675814 + 0.5)
    r = (x - turn * 1.5703125) - turn * 4.838267948966e-4
    z = r * r
    s = r + r * z * (-1.6666654611e-1 + z * (8.3321608736e-3 - z * 1.9515295891e-4))
    c = 1.0 - 0.5 * z + z * z * (4.166664568298827e-2 + z * (-1.388731625493765e-3 + z * 2.443315711809948e-5))
    far = jnp.abs(turn)
    odd = far == 1.0
    sign = jnp.where(far == 2.0, -1.0, 1.0)
    return jnp.where(odd, turn * c, sign * s), jnp.where(odd, -turn * s, sign * c)


def kernel(stages, w_hbm, t_hbm, a_hbm, id_hbm, out, w, mats, ang, ids, cos_tab, sin_tab, cosg, sing,
           send, recv, kept, part, load_sem, send_sem, recv_sem):
    levels = len(stages)
    half = w.shape[2] // 2
    chunks = half // LANES
    boxes = ang.shape[1]

    loads = [pltpu.make_async_copy(src, dst, load_sem.at[n])
             for n, (src, dst) in enumerate(((a_hbm, ang), (id_hbm, ids), (w_hbm, w), (t_hbm, mats)))]
    for load in loads:
        load.start()

    parity, partner = [], []
    for axis, span in stages:
        me = lax.axis_index(axis)
        bit = (me // span) % 2
        parity.append(bit)
        partner.append({axis: me + (1 - 2 * bit) * span})

    barrier = pltpu.get_barrier_semaphore()
    for peer in partner:
        pl.semaphore_signal(barrier, inc=1, device_id=peer, device_id_type=MESH)

    def exchange(level, c):
        return pltpu.make_async_remote_copy(
            src_ref=send.at[level, c], dst_ref=recv.at[level, c],
            send_sem=send_sem.at[level, c], recv_sem=recv_sem.at[level, c],
            device_id=partner[level], device_id_type=MESH)

    def gather(level, h):
        row = ids[level:level + 1, pl.ds(pl.multiple_of(h * half, LANES), half)]
        hot = jnp.where(lax.broadcasted_iota(jnp.int32, (boxes, half), 0) == row, 1.0, 0.0).astype(jnp.bfloat16)
        c_all = jnp.dot(cos_tab[...], hot, preferred_element_type=jnp.float32).astype(jnp.bfloat16)
        s_all = jnp.dot(sin_tab[...], hot, preferred_element_type=jnp.float32).astype(jnp.bfloat16)
        for c in range(chunks):
            cosg[level, h, c] = c_all[:, c * LANES:(c + 1) * LANES]
            sing[level, h, c] = s_all[:, c * LANES:(c + 1) * LANES]

    def rotate(level, h, c, re, im):
        co = cosg[level, h, c].astype(jnp.float32)
        si = sing[level, h, c].astype(jnp.float32)
        return (co * re - si * im).astype(jnp.bfloat16), (si * re + co * im).astype(jnp.bfloat16)

    def put(ref, pair):
        ref[:, :LANES] = pair[0]
        ref[:, LANES:] = pair[1]

    def near(level, c):
        for t in range(2):
            part[c, t] = jnp.dot(mats[t, parity[level]], kept[c], preferred_element_type=jnp.float32)

    def first(h, c):
        cols = pl.ds(pl.multiple_of(h * half + c * LANES, LANES), LANES)
        return rotate(0, h, c, w[0, :, cols].astype(jnp.float32), w[1, :, cols].astype(jnp.float32))

    loads[0].wait()
    sin_v, cos_v = sin_cos(ang[...])
    sin_tab[...] = sin_v.astype(jnp.bfloat16)
    cos_tab[...] = cos_v.astype(jnp.bfloat16)
    loads[1].wait()
    gather(0, 1 - parity[0])
    loads[2].wait()
    for c in range(chunks):
        put(send.at[0, c], first(1 - parity[0], c))
        if c == 0:
            pl.semaphore_wait(barrier, levels)
        exchange(0, c).start()
    gather(0, parity[0])
    loads[3].wait()
    for c in range(chunks):
        put(kept.at[c], first(parity[0], c))
        near(0, c)
    for level in range(1, levels):
        for h in range(2):
            gather(level, h)

    for level in range(levels):
        for c in range(chunks):
            exchange(level, c).wait_recv()
            far = 1 - parity[level]

            def mixed(t):
                y = part[c, t] + jnp.dot(mats[t, far], recv[level, c], preferred_element_type=jnp.float32)
                return y[:, :LANES], y[:, LANES:]

            if level + 1 < levels:
                keep = parity[level + 1]
                put(send.at[level + 1, c], rotate(level + 1, 1 - keep, c, *mixed(1 - keep)))
                exchange(level + 1, c).start()
                put(kept.at[c], rotate(level + 1, keep, c, *mixed(keep)))
                near(level + 1, c)
            else:
                for t in range(2):
                    re, im = mixed(t)
                    cols = slice(t * half + c * LANES, t * half + (c + 1) * LANES)
                    out[0, :, cols] = re.astype(out.dtype)
                    out[1, :, cols] = im.astype(out.dtype)
    for level in range(levels):
        for c in range(chunks):
            exchange(level, c).wait_send()


def shards(stages, weights, translate, angles, box_ids):
    points, cols = weights.shape[1:]
    levels, chunks = len(stages), cols // 2 // LANES
    bf16 = jnp.bfloat16
    return pl.pallas_call(
        functools.partial(kernel, stages),
        out_shape=jax.ShapeDtypeStruct(weights.shape, weights.dtype),
        in_specs=[pl.BlockSpec(memory_space=pl.ANY)] * 4,
        out_specs=pl.BlockSpec(memory_space=pltpu.VMEM),
        scratch_shapes=[
            pltpu.VMEM(weights.shape, bf16),
            pltpu.VMEM(translate.shape, bf16),
            pltpu.VMEM(angles.shape, jnp.float32),
            pltpu.VMEM(box_ids.shape, jnp.int32),
            pltpu.VMEM(angles.shape, bf16),
            pltpu.VMEM(angles.shape, bf16),
            pltpu.VMEM((levels, 2, chunks, points, LANES), bf16),
            pltpu.VMEM((levels, 2, chunks, points, LANES), bf16),
            pltpu.VMEM((levels, chunks, points, 2 * LANES), bf16),
            pltpu.VMEM((levels, chunks, points, 2 * LANES), bf16),
            pltpu.VMEM((chunks, points, 2 * LANES), bf16),
            pltpu.VMEM((chunks, 2, points, 2 * LANES), jnp.float32),
            pltpu.SemaphoreType.DMA((4,)),
            pltpu.SemaphoreType.DMA((levels, chunks)),
            pltpu.SemaphoreType.DMA((levels, chunks)),
        ],
        compiler_params=pltpu.CompilerParams(collective_id=0, has_side_effects=True),
    )(weights, translate, angles, box_ids)


def solution(mesh):
    stages = [(axis, 1 << b) for axis in AXES for b in range(mesh.shape[axis].bit_length() - 1)]
    in_specs = (P(None, None, AXES), P(), P(), P(None, AXES))
    return jax.shard_map(functools.partial(shards, stages), mesh=mesh, in_specs=in_specs,
                         out_specs=P(None, None, AXES), check_vma=False)
```

```python
import functools

import jax
import jax.numpy as jnp
from jax import lax
from jax.experimental import pallas as pl
from jax.experimental.pallas import tpu as pltpu
from jax.sharding import PartitionSpec as P

AXES = ("gx", "gy", "gz")
MESH = pl.DeviceIdType.MESH
LANES = 128


def sin_cos(x):
    turn = jnp.floor(x * 0.6366197723675814 + 0.5)
    r = (x - turn * 1.5703125) - turn * 4.838267948966e-4
    z = r * r
    s = r + r * z * (-1.6666654611e-1 + z * (8.3321608736e-3 - z * 1.9515295891e-4))
    c = 1.0 - 0.5 * z + z * z * (4.166664568298827e-2 + z * (-1.388731625493765e-3 + z * 2.443315711809948e-5))
    far = jnp.abs(turn)
    odd = far == 1.0
    sign = jnp.where(far == 2.0, -1.0, 1.0)
    return jnp.where(odd, turn * c, sign * s), jnp.where(odd, -turn * s, sign * c)


def kernel(stages, w_hbm, t_hbm, a_hbm, id_hbm, out, w, mats, ang, ids, cos_tab, sin_tab, cosg, sing,
           send, recv, kept, part, load_sem, send_sem, recv_sem):
    levels = len(stages)
    half = w.shape[2] // 2
    chunks = half // LANES
    boxes = ang.shape[1]

    loads = [pltpu.make_async_copy(src, dst, load_sem.at[n])
             for n, (src, dst) in enumerate(((a_hbm, ang), (id_hbm, ids), (w_hbm, w), (t_hbm, mats)))]
    for load in loads:
        load.start()

    parity, partner = [], []
    for axis, span in stages:
        me = lax.axis_index(axis)
        bit = (me // span) % 2
        parity.append(bit)
        partner.append({axis: me + (1 - 2 * bit) * span})

    barrier = pltpu.get_barrier_semaphore()
    for peer in partner:
        pl.semaphore_signal(barrier, inc=1, device_id=peer, device_id_type=MESH)

    def exchange(level, c):
        return pltpu.make_async_remote_copy(
            src_ref=send.at[level, c], dst_ref=recv.at[level, c],
            send_sem=send_sem.at[level, c], recv_sem=recv_sem.at[level, c],
            device_id=partner[level], device_id_type=MESH)

    def gather(level, h):
        row = ids[level:level + 1, pl.ds(pl.multiple_of(h * half, LANES), half)]
        hot = jnp.where(lax.broadcasted_iota(jnp.int32, (boxes, half), 0) == row, 1.0, 0.0).astype(jnp.bfloat16)
        c_all = jnp.dot(cos_tab[...], hot, preferred_element_type=jnp.float32).astype(jnp.bfloat16)
        s_all = jnp.dot(sin_tab[...], hot, preferred_element_type=jnp.float32).astype(jnp.bfloat16)
        for c in range(chunks):
            cosg[level, h, c] = c_all[:, c * LANES:(c + 1) * LANES]
            sing[level, h, c] = s_all[:, c * LANES:(c + 1) * LANES]

    def rotate(level, h, c, re, im):
        co = cosg[level, h, c].astype(jnp.float32)
        si = sing[level, h, c].astype(jnp.float32)
        return (co * re - si * im).astype(jnp.bfloat16), (si * re + co * im).astype(jnp.bfloat16)

    def put(ref, pair):
        ref[:, :LANES] = pair[0]
        ref[:, LANES:] = pair[1]

    def near(level, c):
        for t in range(2):
            part[c, t] = jnp.dot(mats[t, parity[level]], kept[c], preferred_element_type=jnp.float32)

    def first(h, c):
        cols = pl.ds(pl.multiple_of(h * half + c * LANES, LANES), LANES)
        return rotate(0, h, c, w[0, :, cols].astype(jnp.float32), w[1, :, cols].astype(jnp.float32))

    loads[0].wait()
    sin_v, cos_v = sin_cos(ang[...])
    sin_tab[...] = sin_v.astype(jnp.bfloat16)
    cos_tab[...] = cos_v.astype(jnp.bfloat16)
    loads[1].wait()
    gather(0, 1 - parity[0])
    loads[2].wait()
    for c in range(chunks):
        put(send.at[0, c], first(1 - parity[0], c))
        if c == 0:
            pl.semaphore_wait(barrier, levels)
        exchange(0, c).start()
    gather(0, parity[0])
    loads[3].wait()
    for c in range(chunks):
        put(kept.at[c], first(parity[0], c))
        near(0, c)
    for level in range(1, levels):
        for h in range(2):
            gather(level, h)

    for level in range(levels):
        for c in range(chunks):
            exchange(level, c).wait_recv()
            far = 1 - parity[level]

            def mixed(t):
                y = part[c, t] + jnp.dot(mats[t, far], recv[level, c], preferred_element_type=jnp.float32)
                return y[:, :LANES], y[:, LANES:]

            if level + 1 < levels:
                keep = parity[level + 1]
                put(send.at[level + 1, c], rotate(level + 1, 1 - keep, c, *mixed(1 - keep)))
                exchange(level + 1, c).start()
                put(kept.at[c], rotate(level + 1, keep, c, *mixed(keep)))
                near(level + 1, c)
            else:
                for t in range(2):
                    re, im = mixed(t)
                    cols = slice(t * half + c * LANES, t * half + (c + 1) * LANES)
                    out[0, :, cols] = re.astype(out.dtype)
                    out[1, :, cols] = im.astype(out.dtype)
    for level in range(levels):
        for c in range(chunks):
            exchange(level, c).wait_send()


def shards(stages, weights, translate, angles, box_ids):
    points, cols = weights.shape[1:]
    levels, chunks = len(stages), cols // 2 // LANES
    bf16 = jnp.bfloat16
    return pl.pallas_call(
        functools.partial(kernel, stages),
        out_shape=pltpu.VMEM(weights.shape, weights.dtype),
        in_specs=[pl.BlockSpec(memory_space=pl.ANY)] * 4,
        out_specs=pl.BlockSpec(memory_space=pltpu.VMEM),
        scratch_shapes=[
            pltpu.VMEM(weights.shape, bf16),
            pltpu.VMEM(translate.shape, bf16),
            pltpu.VMEM(angles.shape, jnp.float32),
            pltpu.VMEM(box_ids.shape, jnp.int32),
            pltpu.VMEM(angles.shape, bf16),
            pltpu.VMEM(angles.shape, bf16),
            pltpu.VMEM((levels, 2, chunks, points, LANES), bf16),
            pltpu.VMEM((levels, 2, chunks, points, LANES), bf16),
            pltpu.VMEM((levels, chunks, points, 2 * LANES), bf16),
            pltpu.VMEM((levels, chunks, points, 2 * LANES), bf16),
            pltpu.VMEM((chunks, points, 2 * LANES), bf16),
            pltpu.VMEM((chunks, 2, points, 2 * LANES), jnp.float32),
            pltpu.SemaphoreType.DMA((4,)),
            pltpu.SemaphoreType.DMA((levels, chunks)),
            pltpu.SemaphoreType.DMA((levels, chunks)),
        ],
        compiler_params=pltpu.CompilerParams(collective_id=0, has_side_effects=True),
    )(weights, translate, angles, box_ids)


def solution(mesh):
    stages = [(axis, 1 << b) for axis in AXES for b in range(mesh.shape[axis].bit_length() - 1)]
    in_specs = (P(None, None, AXES), P(), P(), P(None, AXES))
    return jax.shard_map(functools.partial(shards, stages), mesh=mesh, in_specs=in_specs,
                         out_specs=P(None, None, AXES), check_vma=False)
```

```python
import functools

import jax
import jax.numpy as jnp
from jax import lax
from jax.experimental import pallas as pl
from jax.experimental.pallas import tpu as pltpu
from jax.sharding import PartitionSpec as P

AXES = ("gx", "gy", "gz")
MESH = pl.DeviceIdType.MESH
LANES = 128
WIDTH = LANES // 2


def sin_cos(x):
    turn = jnp.floor(x * 0.6366197723675814 + 0.5)
    r = (x - turn * 1.5703125) - turn * 4.838267948966e-4
    z = r * r
    s = r + r * z * (-1.6666654611e-1 + z * (8.3321608736e-3 - z * 1.9515295891e-4))
    c = 1.0 - 0.5 * z + z * z * (4.166664568298827e-2 + z * (-1.388731625493765e-3 + z * 2.443315711809948e-5))
    far = jnp.abs(turn)
    odd = far == 1.0
    sign = jnp.where(far == 2.0, -1.0, 1.0)
    return jnp.where(odd, turn * c, sign * s), jnp.where(odd, -turn * s, sign * c)


def kernel(stages, w_hbm, t_hbm, a_hbm, id_hbm, out, w, mats, ang, ids, cos_tab, sin_tab, cosg, sing,
           send, recv, kept, part, load_sem, send_sem, recv_sem):
    levels = len(stages)
    half = w.shape[2] // 2
    points, boxes = ang.shape
    chunks = half // WIDTH

    loads = [pltpu.make_async_copy(src, dst, load_sem.at[n])
             for n, (src, dst) in enumerate(((a_hbm, ang), (id_hbm, ids), (w_hbm, w), (t_hbm, mats)))]
    for load in loads:
        load.start()

    parity, partner = [], []
    for axis, span in stages:
        me = lax.axis_index(axis)
        bit = (me // span) % 2
        parity.append(bit)
        partner.append({axis: me + (1 - 2 * bit) * span})

    barrier = pltpu.get_barrier_semaphore()
    for peer in partner:
        pl.semaphore_signal(barrier, inc=1, device_id=peer, device_id_type=MESH)

    def low(rows):
        return lax.broadcasted_iota(jnp.int32, (rows, LANES), 1) < WIDTH

    def swap(x):
        return pltpu.roll(x, WIDTH, 1)

    def exchange(level, q):
        return pltpu.make_async_remote_copy(
            src_ref=send.at[level, q], dst_ref=recv.at[level, q],
            send_sem=send_sem.at[level, q], recv_sem=recv_sem.at[level, q],
            device_id=partner[level], device_id_type=MESH)

    def columns(h, g):
        return pl.ds(pl.multiple_of(h * half + g * LANES, LANES), LANES)

    def gather(level, h, groups):
        rows = []
        for g in groups:
            row = jnp.broadcast_to(ids[level:level + 1, columns(h, g)], (8, LANES))
            turned = swap(row)
            rows += [jnp.where(low(8), row, turned)[:1], jnp.where(low(8), turned, row)[:1]]
        row = jnp.concatenate(rows, axis=1)
        hot = jnp.where(lax.broadcasted_iota(jnp.int32, (boxes, row.shape[1]), 0) == row, 1.0, 0.0).astype(jnp.bfloat16)
        c_all = jnp.dot(cos_tab[...], hot, preferred_element_type=jnp.float32)
        s_all = jnp.dot(sin_tab[...], hot, preferred_element_type=jnp.float32)
        for n in range(len(rows)):
            q = 2 * groups[0] + n
            cols = slice(n * LANES, (n + 1) * LANES)
            cosg[level, h, q] = c_all[:, cols].astype(jnp.bfloat16)
            sing[level, h, q] = jnp.where(low(points), -s_all[:, cols], s_all[:, cols]).astype(jnp.bfloat16)

    def rotate(level, h, q, x):
        co = cosg[level, h, q].astype(jnp.float32)
        si = sing[level, h, q].astype(jnp.float32)
        return (co * x + si * swap(x)).astype(jnp.bfloat16)

    def near(level, q):
        for t in range(2):
            part[q, t] = jnp.dot(mats[t, parity[level]], kept[q], preferred_element_type=jnp.float32)

    def first(h, g):
        re = w[0, :, columns(h, g)].astype(jnp.float32)
        im = w[1, :, columns(h, g)].astype(jnp.float32)
        pair = jnp.where(low(points), re, swap(im)), jnp.where(low(points), swap(re), im)
        return [(2 * g + side, rotate(0, h, 2 * g + side, x)) for side, x in enumerate(pair)]

    groups = list(range(chunks // 2))
    loads[0].wait()
    sin_v, cos_v = sin_cos(ang[...])
    sin_tab[...] = sin_v.astype(jnp.bfloat16)
    cos_tab[...] = cos_v.astype(jnp.bfloat16)
    loads[1].wait()
    for g in groups:
        gather(0, 1 - parity[0], [g])
        if g == 0:
            loads[2].wait()
        for q, x in first(1 - parity[0], g):
            send[0, q] = x
        if g == 0:
            pl.semaphore_wait(barrier, levels)
        for side in range(2):
            exchange(0, 2 * g + side).start()
    gather(0, parity[0], groups)
    loads[3].wait()
    for g in groups:
        for q, x in first(parity[0], g):
            kept[q] = x
            near(0, q)
    for level in range(1, levels):
        for h in range(2):
            gather(level, h, groups)

    ready = set()
    for level, q in [(level, q) for level in range(levels) for q in range(chunks)]:
        far = 1 - parity[level]
        exchange(level, q).wait_recv()

        def mixed(t):
            return part[q, t] + jnp.dot(mats[t, far], recv[level, q], preferred_element_type=jnp.float32)

        if level + 1 < levels:
            keep = parity[level + 1]
            send[level + 1, q] = rotate(level + 1, 1 - keep, q, mixed(1 - keep))
            exchange(level + 1, q).start()
            kept[q] = rotate(level + 1, keep, q, mixed(keep))
            near(level + 1, q)
        else:
            for t in range(2):
                y = mixed(t)
                if q ^ 1 in ready:
                    other = part[q ^ 1, t]
                    a, b = (other, y) if q % 2 else (y, other)
                    cols = slice(t * half + q // 2 * LANES, t * half + (q // 2 + 1) * LANES)
                    out[0, :, cols] = jnp.where(low(points), a, swap(b)).astype(out.dtype)
                    out[1, :, cols] = jnp.where(low(points), swap(a), b).astype(out.dtype)
                else:
                    part[q, t] = y
            ready.add(q)
    for level in range(levels):
        for q in range(chunks):
            exchange(level, q).wait_send()


def shards(stages, weights, translate, angles, box_ids):
    points, cols = weights.shape[1:]
    levels, chunks = len(stages), cols // 2 // WIDTH
    bf16 = jnp.bfloat16
    return pl.pallas_call(
        functools.partial(kernel, stages),
        out_shape=pltpu.VMEM(weights.shape, weights.dtype),
        in_specs=[pl.BlockSpec(memory_space=pl.ANY)] * 4,
        out_specs=pl.BlockSpec(memory_space=pltpu.VMEM),
        scratch_shapes=[
            pltpu.VMEM(weights.shape, bf16),
            pltpu.VMEM(translate.shape, bf16),
            pltpu.VMEM(angles.shape, jnp.float32),
            pltpu.VMEM(box_ids.shape, jnp.int32),
            pltpu.VMEM(angles.shape, bf16),
            pltpu.VMEM(angles.shape, bf16),
            pltpu.VMEM((levels, 2, chunks, points, LANES), bf16),
            pltpu.VMEM((levels, 2, chunks, points, LANES), bf16),
            pltpu.VMEM((levels, chunks, points, LANES), bf16),
            pltpu.VMEM((levels, chunks, points, LANES), bf16),
            pltpu.VMEM((chunks, points, LANES), bf16),
            pltpu.VMEM((chunks, 2, points, LANES), jnp.float32),
            pltpu.SemaphoreType.DMA((4,)),
            pltpu.SemaphoreType.DMA((levels, chunks)),
            pltpu.SemaphoreType.DMA((levels, chunks)),
        ],
        compiler_params=pltpu.CompilerParams(collective_id=0, has_side_effects=True),
    )(weights, translate, angles, box_ids)


def solution(mesh):
    stages = [(axis, 1 << b) for axis in AXES for b in range(mesh.shape[axis].bit_length() - 1)]
    in_specs = (P(None, None, AXES), P(), P(), P(None, AXES))
    return jax.shard_map(functools.partial(shards, stages), mesh=mesh, in_specs=in_specs,
                         out_specs=P(None, None, AXES), check_vma=False)
```

```python
import functools

import jax
import jax.numpy as jnp
from jax import lax
from jax.experimental import pallas as pl
from jax.experimental.pallas import tpu as pltpu
from jax.sharding import PartitionSpec as P

AXES = ("gx", "gy", "gz")
MESH = pl.DeviceIdType.MESH
LANES = 128
WIDTH = LANES // 2


def sin_cos(x):
    turn = jnp.floor(x * 0.6366197723675814 + 0.5)
    r = (x - turn * 1.5703125) - turn * 4.838267948966e-4
    z = r * r
    s = r + r * z * (-1.6666654611e-1 + z * (8.3321608736e-3 - z * 1.9515295891e-4))
    c = 1.0 - 0.5 * z + z * z * (4.166664568298827e-2 + z * (-1.388731625493765e-3 + z * 2.443315711809948e-5))
    far = jnp.abs(turn)
    odd = far == 1.0
    sign = jnp.where(far == 2.0, -1.0, 1.0)
    return jnp.where(odd, turn * c, sign * s), jnp.where(odd, -turn * s, sign * c)


def kernel(stages, w_hbm, t_hbm, a_hbm, id_hbm, out, w, mats, ang, ids, cos_tab, sin_tab, cosg, sing,
           send, recv, kept, part, load_sem, send_sem, recv_sem):
    levels = len(stages)
    half = w.shape[2] // 2
    points, boxes = ang.shape
    chunks = half // WIDTH

    loads = [pltpu.make_async_copy(src, dst, load_sem.at[n])
             for n, (src, dst) in enumerate(((a_hbm, ang), (id_hbm, ids), (w_hbm, w), (t_hbm, mats)))]
    for load in loads:
        load.start()

    parity, partner = [], []
    for axis, span in stages:
        me = lax.axis_index(axis)
        bit = (me // span) % 2
        parity.append(bit)
        partner.append({axis: me + (1 - 2 * bit) * span})

    barrier = pltpu.get_barrier_semaphore()
    for peer in partner:
        pl.semaphore_signal(barrier, inc=1, device_id=peer, device_id_type=MESH)

    def low(rows):
        return lax.broadcasted_iota(jnp.int32, (rows, LANES), 1) < WIDTH

    def swap(x):
        return pltpu.roll(x, WIDTH, 1)

    def exchange(level, q):
        return pltpu.make_async_remote_copy(
            src_ref=send.at[level, q], dst_ref=recv.at[level, q],
            send_sem=send_sem.at[level, q], recv_sem=recv_sem.at[level, q],
            device_id=partner[level], device_id_type=MESH)

    def columns(h, g):
        return pl.ds(pl.multiple_of(h * half + g * LANES, LANES), LANES)

    def gather(level, h, groups):
        rows = []
        for g in groups:
            row = jnp.broadcast_to(ids[level:level + 1, columns(h, g)], (8, LANES))
            turned = swap(row)
            rows += [jnp.where(low(8), row, turned)[:1], jnp.where(low(8), turned, row)[:1]]
        row = jnp.concatenate(rows, axis=1)
        hot = jnp.where(lax.broadcasted_iota(jnp.int32, (boxes, row.shape[1]), 0) == row, 1.0, 0.0).astype(jnp.bfloat16)
        c_all = jnp.dot(cos_tab[...], hot, preferred_element_type=jnp.float32)
        s_all = jnp.dot(sin_tab[...], hot, preferred_element_type=jnp.float32)
        for n in range(len(rows)):
            q = 2 * groups[0] + n
            cols = slice(n * LANES, (n + 1) * LANES)
            cosg[level, h, q] = c_all[:, cols].astype(jnp.bfloat16)
            sing[level, h, q] = jnp.where(low(points), -s_all[:, cols], s_all[:, cols]).astype(jnp.bfloat16)

    def rotate(level, h, q, x):
        co = cosg[level, h, q].astype(jnp.float32)
        si = sing[level, h, q].astype(jnp.float32)
        return (co * x + si * swap(x)).astype(jnp.bfloat16)

    def near(level, q):
        for t in range(2):
            part[q, t] = jnp.dot(mats[t, parity[level]], kept[q], preferred_element_type=jnp.float32)

    def first(h, g):
        re = w[0, :, columns(h, g)].astype(jnp.float32)
        im = w[1, :, columns(h, g)].astype(jnp.float32)
        pair = jnp.where(low(points), re, swap(im)), jnp.where(low(points), swap(re), im)
        return [(2 * g + side, rotate(0, h, 2 * g + side, x)) for side, x in enumerate(pair)]

    groups = list(range(chunks // 2))
    loads[0].wait()
    sin_v, cos_v = sin_cos(ang[...])
    sin_tab[...] = sin_v.astype(jnp.bfloat16)
    cos_tab[...] = cos_v.astype(jnp.bfloat16)
    loads[1].wait()
    for g in groups:
        gather(0, 1 - parity[0], [g])
        if g == 0:
            loads[2].wait()
        for q, x in first(1 - parity[0], g):
            send[0, q] = x
        if g == 0:
            pl.semaphore_wait(barrier, levels)
        for side in range(2):
            exchange(0, 2 * g + side).start()
    gather(0, parity[0], groups)
    loads[3].wait()
    for g in groups:
        for q, x in first(parity[0], g):
            kept[q] = x
            near(0, q)
    for level in range(1, levels):
        for h in range(2):
            gather(level, h, groups)

    ready = set()
    steps = [(level, q) for level in range(levels) for q in range(chunks)]
    for level, q in sorted(steps, key=lambda step: (2 * step[0] + step[1], -step[0])):
        far = 1 - parity[level]
        exchange(level, q).wait_recv()

        def mixed(t):
            return part[q, t] + jnp.dot(mats[t, far], recv[level, q], preferred_element_type=jnp.float32)

        if level + 1 < levels:
            keep = parity[level + 1]
            send[level + 1, q] = rotate(level + 1, 1 - keep, q, mixed(1 - keep))
            exchange(level + 1, q).start()
            kept[q] = rotate(level + 1, keep, q, mixed(keep))
            near(level + 1, q)
        else:
            for t in range(2):
                y = mixed(t)
                if q ^ 1 in ready:
                    other = part[q ^ 1, t]
                    a, b = (other, y) if q % 2 else (y, other)
                    cols = slice(t * half + q // 2 * LANES, t * half + (q // 2 + 1) * LANES)
                    out[0, :, cols] = jnp.where(low(points), a, swap(b)).astype(out.dtype)
                    out[1, :, cols] = jnp.where(low(points), swap(a), b).astype(out.dtype)
                else:
                    part[q, t] = y
            ready.add(q)
    for level in range(levels):
        for q in range(chunks):
            exchange(level, q).wait_send()


def shards(stages, weights, translate, angles, box_ids):
    points, cols = weights.shape[1:]
    levels, chunks = len(stages), cols // 2 // WIDTH
    bf16 = jnp.bfloat16
    return pl.pallas_call(
        functools.partial(kernel, stages),
        out_shape=pltpu.VMEM(weights.shape, weights.dtype),
        in_specs=[pl.BlockSpec(memory_space=pl.ANY)] * 4,
        out_specs=pl.BlockSpec(memory_space=pltpu.VMEM),
        scratch_shapes=[
            pltpu.VMEM(weights.shape, bf16),
            pltpu.VMEM(translate.shape, bf16),
            pltpu.VMEM(angles.shape, jnp.float32),
            pltpu.VMEM(box_ids.shape, jnp.int32),
            pltpu.VMEM(angles.shape, bf16),
            pltpu.VMEM(angles.shape, bf16),
            pltpu.VMEM((levels, 2, chunks, points, LANES), bf16),
            pltpu.VMEM((levels, 2, chunks, points, LANES), bf16),
            pltpu.VMEM((levels, chunks, points, LANES), bf16),
            pltpu.VMEM((levels, chunks, points, LANES), bf16),
            pltpu.VMEM((chunks, points, LANES), bf16),
            pltpu.VMEM((chunks, 2, points, LANES), jnp.float32),
            pltpu.SemaphoreType.DMA((4,)),
            pltpu.SemaphoreType.DMA((levels, chunks)),
            pltpu.SemaphoreType.DMA((levels, chunks)),
        ],
        compiler_params=pltpu.CompilerParams(collective_id=0, has_side_effects=True),
    )(weights, translate, angles, box_ids)


def solution(mesh):
    stages = [(axis, 1 << b) for axis in AXES for b in range(mesh.shape[axis].bit_length() - 1)]
    in_specs = (P(None, None, AXES), P(), P(), P(None, AXES))
    return jax.shard_map(functools.partial(shards, stages), mesh=mesh, in_specs=in_specs,
                         out_specs=P(None, None, AXES), check_vma=False)
```
